256 devices in a mesh: narrow: 16 (over z, core), wide: 16 (over x, y).
Axes of the slice: x: 4, y: 4, z: 8, core: 2. Of those that a mesh axis runs over, the one named last changes fastest.
Arguments:
- inputs: bfloat16 [2048, 8192], P('narrow', 'wide'), may hold values from -6 to 6
- gate_blocks: bfloat16 [112, 16, 128, 128], P('wide', 'narrow'), may hold values from -0.125 to 0.125
- up_blocks: bfloat16 [112, 16, 128, 128], P('wide', 'narrow'), may hold values from -0.125 to 0.125
- pattern: int32 [112, 16], P('wide'), may hold values from 0 to 63, as said below
- grad_hidden: bfloat16 [2048, 14336], P('narrow', 'wide'), may hold values from -0.59765625 to 0.59765625
Outputs:
- hidden: bfloat16 [2048, 14336], P('narrow', 'wide')
- grad_inputs: bfloat16 [2048, 8192], P('narrow', 'wide')
- grad_gate: bfloat16 [112, 16, 128, 128], P('wide', 'narrow')
- grad_up: bfloat16 [112, 16, 128, 128], P('wide', 'narrow')
The draws below stay inside these ranges and needn't reach their ends.
Inputs may be any that keep to these rules, and one draw needn't show every extreme that they name: pattern[j, k] = b_j XOR m_k, with one offset b_j for each block column and 16 distinct masks m_k common to all block columns, so each block column lists 16 distinct block rows.
All inputs are finite; a program needn't handle non-finite values.
Results may differ from the reference program's by a relative error of at most 0.023.
Values may be sent and summed in bfloat16 or wider, within the bound.
A program may use at most 128 MiB of HBM per device.

```python
import jax
import jax.numpy as jnp
from jax import lax

D = 8192
FF = 14336
BLK = 128
TOK_DEV = 128
FB = 112
NZ = 16
TOKENS = 2048
N_NARROW = 16
N_WIDE = 16


def draw_pattern(key, part):
    row_blocks = D // BLK
    slots = row_blocks // 4
    columns = FF // BLK
    key_rank, key_base = jax.random.split(key)
    ranking = jax.random.permutation(key_rank, row_blocks).astype(jnp.int32)
    numbers = jnp.arange(row_blocks, dtype=jnp.int32)
    butterfly = jnp.bitwise_and(numbers, numbers - 1) == 0
    scores = jnp.where(butterfly, ranking, row_blocks + ranking)
    masks = jnp.argsort(scores)[:slots].astype(jnp.int32)
    offset = jax.random.randint(key_base, (), 0, row_blocks, dtype=jnp.int32)
    column_base = jnp.bitwise_xor(jnp.arange(columns, dtype=jnp.int32) % row_blocks, offset)
    return jnp.bitwise_xor(column_base[:, None], masks[None, :]).astype(jnp.int32)


def levels(own_key, shape, cuts, least, high):
    def one(position, shards_of):
        draws = jax.random.uniform(jax.random.fold_in(jax.random.fold_in(own_key, 6), position), (shards_of,), jnp.float32, least / len(cuts), high / len(cuts))
        return jnp.repeat(jnp.exp(draws), shape[position] // shards_of).reshape((-1,) + (1,) * (len(shape) - position - 1))

    level = one(*cuts[0])
    for cut in cuts[1:]:
        level = level * one(*cut)
    return level


def bell_draw(stream_key, extent, scale, reach, cuts=(), kind=jnp.bfloat16):
    loudness = levels(stream_key, extent, cuts, -0.22, 0.18) if cuts else 1.0
    values = jax.random.normal(stream_key, extent, jnp.float32) * scale * loudness
    return jnp.minimum(jnp.maximum(values, -reach), reach).astype(kind)


def setup_inputs(seed: int = 0) -> dict:
    splits = jax.random.split(jax.random.key(seed), 6)
    return {
        "inputs": bell_draw(splits[0], (TOKENS, D), 1.0, 6.0, ((0, 16), (1, 16))),
        "gate_blocks": bell_draw(splits[1], (FB, NZ, BLK, BLK), (NZ * BLK) ** -0.5, 0.125, ((0, 16), (1, 16))),
        "up_blocks": bell_draw(splits[2], (FB, NZ, BLK, BLK), (NZ * BLK) ** -0.5, 0.125, ((0, 16), (1, 16))),
        "pattern": draw_pattern(jax.random.fold_in(splits[5], 71), 0),
        "grad_hidden": bell_draw(splits[4], (TOKENS, FF), 0.1, 0.59765625, ((0, 16), (1, 16))),
    }


def silu_parts(gate_sum):
    sigmoid_value = jax.nn.sigmoid(gate_sum)
    return gate_sum * sigmoid_value, sigmoid_value * (1.0 + gate_sum * (1.0 - sigmoid_value))


def rounded(values):
    return lax.optimization_barrier(values.astype(jnp.bfloat16)).astype(jnp.float32)


def reference(inputs, gate_blocks, up_blocks, pattern, grad_hidden):
    row_blocks = D // BLK
    columns = FF // BLK
    slots = row_blocks // 4
    group_columns = columns // N_WIDE
    token_groups = inputs.reshape(N_NARROW, TOK_DEV, row_blocks, BLK)
    cotangent_groups = grad_hidden.reshape(N_NARROW, TOK_DEV, columns, BLK)
    gate_weights = gate_blocks.astype(jnp.float32)
    up_weights = up_blocks.astype(jnp.float32)
    wide_ids = jnp.arange(N_WIDE, dtype=jnp.int32)[:, None, None]
    wide_pattern = pattern.reshape(N_WIDE, group_columns, slots)

    def one_group(totals, group_item):
        group_inputs, group_cotangent = group_item
        picked = group_inputs[:, pattern].astype(jnp.float32)
        gate_sum = jnp.einsum('tjkb,jkbc->tjc', picked, gate_weights)
        up_sum = jnp.einsum('tjkb,jkbc->tjc', picked, up_weights)
        activation, derivative = silu_parts(gate_sum)
        hidden = (activation * up_sum).astype(jnp.bfloat16)
        cotangent = group_cotangent.astype(jnp.float32)
        d_gate = rounded(cotangent * up_sum * derivative)
        d_up = rounded(cotangent * activation)
        contribution = jnp.einsum('tjc,jkbc->tjkb', d_gate, gate_weights) + jnp.einsum('tjc,jkbc->tjkb', d_up, up_weights)
        shaped = contribution.reshape(TOK_DEV, N_WIDE, group_columns, slots, BLK).transpose(1, 2, 3, 0, 4)
        scattered = jnp.zeros((N_WIDE, row_blocks, TOK_DEV, BLK), jnp.float32).at[wide_ids, wide_pattern].add(shaped)
        grad_group = jnp.sum(rounded(scattered), axis=0).transpose(1, 0, 2).reshape(TOK_DEV, D).astype(jnp.bfloat16)
        gate_term = rounded(jnp.einsum('tjkb,tjc->jkbc', picked, d_gate))
        up_term = rounded(jnp.einsum('tjkb,tjc->jkbc', picked, d_up))
        return (totals[0] + gate_term, totals[1] + up_term), (hidden.reshape(TOK_DEV, FF), grad_group)

    zero_grads = jnp.zeros((columns, slots, BLK, BLK), jnp.float32)
    totals, outputs = lax.scan(one_group, (zero_grads, zero_grads), (token_groups, cotangent_groups))
    hiddens, grads = outputs
    return (hiddens.reshape(TOKENS, FF), grads.reshape(TOKENS, D), totals[0].astype(jnp.bfloat16), totals[1].astype(jnp.bfloat16))
```

```python
import functools

import jax
import jax.numpy as jnp
from jax import lax
from jax.experimental import pallas as pl
from jax.experimental.pallas import tpu as pltpu
from jax.sharding import PartitionSpec as P


def layer_kernel(pat_ref, x_ref, w_ref, gh_ref, hid_ref, gin_ref, gw_ref, acc_ref):
    columns, slots = pat_ref.shape
    blk = w_ref.shape[-1]
    acc_ref[...] = jnp.zeros_like(acc_ref)

    def one_column(j, carry):
        def fwd(k, sums):
            g, u = sums
            r = pat_ref[j, k]
            xb = x_ref[:, pl.ds(pl.multiple_of(r * blk, blk), blk)]
            g = g + jnp.dot(xb, w_ref[0, j, k], preferred_element_type=jnp.float32)
            u = u + jnp.dot(xb, w_ref[1, j, k], preferred_element_type=jnp.float32)
            return g, u

        zero = jnp.zeros((x_ref.shape[0], blk), jnp.float32)
        g, u = lax.fori_loop(0, slots, fwd, (zero, zero))
        s = jax.nn.sigmoid(g)
        act = g * s
        deriv = s * (1.0 + g * (1.0 - s))
        cols = pl.ds(pl.multiple_of(j * blk, blk), blk)
        hid_ref[:, cols] = (act * u).astype(hid_ref.dtype)
        cot = gh_ref[:, cols].astype(jnp.float32)
        dg = (cot * u * deriv).astype(jnp.bfloat16)
        du = (cot * act).astype(jnp.bfloat16)

        def bwd(k, c):
            r = pat_ref[j, k]
            rows = pl.ds(pl.multiple_of(r * blk, blk), blk)
            xb = x_ref[:, rows]
            nt = (((1,), (1,)), ((), ()))
            contrib = lax.dot_general(dg, w_ref[0, j, k], nt, preferred_element_type=jnp.float32)
            contrib = contrib + lax.dot_general(du, w_ref[1, j, k], nt, preferred_element_type=jnp.float32)
            acc_ref[:, rows] += contrib
            tn = (((0,), (0,)), ((), ()))
            gw_ref[k, 0, j] = lax.dot_general(xb, dg, tn, preferred_element_type=jnp.float32).astype(gw_ref.dtype)
            gw_ref[k, 1, j] = lax.dot_general(xb, du, tn, preferred_element_type=jnp.float32).astype(gw_ref.dtype)
            return c

        lax.fori_loop(0, slots, bwd, 0)
        return carry

    lax.fori_loop(0, columns, one_column, 0)
    gin_ref[...] = acc_ref[...].astype(gin_ref.dtype)


def local_layer(x_full, w_all, pattern, grad_hidden):
    tokens, width = x_full.shape
    _, columns, slots, blk, _ = w_all.shape
    vmem = pl.BlockSpec(memory_space=pltpu.VMEM)
    flops = 2 * tokens * columns * slots * blk * blk * 6
    return pl.pallas_call(
        layer_kernel,
        out_shape=(
            jax.ShapeDtypeStruct((tokens, columns * blk), jnp.bfloat16),
            jax.ShapeDtypeStruct((tokens, width), jnp.bfloat16),
            jax.ShapeDtypeStruct((slots, 2, columns, blk, blk), jnp.bfloat16),
        ),
        in_specs=[pl.BlockSpec(memory_space=pltpu.SMEM), vmem, vmem, vmem],
        out_specs=(vmem, vmem, vmem),
        scratch_shapes=[pltpu.VMEM((tokens, width), jnp.float32)],
        compiler_params=pltpu.CompilerParams(vmem_limit_bytes=60 * 1024 * 1024),
        cost_estimate=pl.CostEstimate(
            flops=flops, transcendentals=tokens * columns * blk,
            bytes_accessed=2 * (x_full.size * 2 + w_all.size * 2)),
    )(pattern, x_full, w_all, grad_hidden)


def shards(inputs, gate_blocks, up_blocks, pattern, grad_hidden):
    x_full = lax.all_gather(inputs, "wide", axis=1, tiled=True)
    w_local = jnp.stack([gate_blocks, up_blocks])
    w_all = lax.all_gather(w_local, "narrow", axis=2, tiled=True)
    hidden, gin_partial, gw_terms = local_layer(x_full, w_all, pattern, grad_hidden)
    grad_inputs = lax.psum_scatter(gin_partial, "wide", scatter_dimension=1, tiled=True)
    gw = lax.psum_scatter(gw_terms, "narrow", scatter_dimension=0, tiled=True)
    grad_gate = gw[:, 0].transpose(1, 0, 2, 3)
    grad_up = gw[:, 1].transpose(1, 0, 2, 3)
    return hidden, grad_inputs, grad_gate, grad_up


def solution(mesh):
    placed = (
        P("narrow", "wide"),
        P("wide", "narrow", None, None),
        P("wide", "narrow", None, None),
        P("wide", None),
        P("narrow", "wide"),
    )
    return jax.shard_map(
        shards,
        mesh=mesh,
        in_specs=placed,
        out_specs=(
            P("narrow", "wide"),
            P("narrow", "wide"),
            P("wide", "narrow", None, None),
            P("wide", "narrow", None, None),
        ),
        check_vma=False,
    )
```
